768 devices in a mesh: dom: 192 (over z, y, core), grid: 4 (over x).
Axes of the slice: x: 4, y: 8, z: 12, core: 2. Of those that a mesh axis runs over, the one named last changes fastest.
Arguments:
- rhs: bfloat16 [4, 1152, 16, 320], P('grid', 'dom'), may hold values from -24 to 24
- blocks: bfloat16 [4, 1152, 3, 320, 320], P('grid', 'dom'), may hold values from -0.1875 to 0.1875
- offsets: int32 [4, 1152, 3], P('grid', 'dom'), may hold values from -1 to 1
- donor_elem: int32 [4, 192, 4, 2], P('grid', 'dom'), may hold values from 0 to 5
- fringe_elem: int32 [4, 192, 4, 2], P('grid', 'dom'), may hold values from 0 to 5
- donor_weight: float32 [4, 192, 4, 2], P('grid', 'dom'), may hold values from 0.25 to 1
- fringe_count: int32 [4, 192, 4], P('grid', 'dom'), may hold values from 0 to 2, as said below
Outputs:
- powers: bfloat16 [4, 1152, 4, 16, 320], P('grid', 'dom')
- r_factor: float32 [80, 80], replicated
The draws below stay inside these ranges and needn't reach their ends.
Inputs may be any that keep to these rules, and one draw needn't show every extreme that they name: `fringe_count`: the count from a grid to its own partitions is 0. In every draw some partition of each grid receives 2 slots from every other grid.
All inputs are finite; a program needn't handle non-finite values.
Results may differ from the reference program's by a relative error of at most 0.0033.
The reference program's roundings to bfloat16 on the way count: a program that leaves them out, or rounds other values in their place, can miss the bound.
Values may be sent and summed in bfloat16 or wider, within the bound.
A program may use at most 32 MiB of HBM per device.

```python
import jax
import jax.numpy as jnp
from jax import lax

W = 320
R = 16
S = 4
NB = 3
H = 1
C = 2
E = 6
GRIDS = 4
PARTS_SIZE = 192
ELEMS = 1152
COLS = 80


def draw_rhs(key, part):
    position = jnp.arange(ELEMS, dtype=jnp.float32) / max(ELEMS - 1, 1)
    rising = 1.0 + 2.0 * position
    grid_rise = 1.0 + jnp.arange(GRIDS, dtype=jnp.float32) / max(GRIDS - 1, 1)
    profile = grid_rise[:, None, None, None] * rising[None, :, None, None]
    values = jnp.clip(jax.random.normal(key, (GRIDS, ELEMS, R, W), jnp.float32), -4.0, 4.0)
    return jnp.clip(values * profile, -24.0, 24.0).astype(jnp.bfloat16)


def draw_fringe_count(key, part):
    counts = jax.random.randint(key, (GRIDS, PARTS_SIZE, GRIDS), 0, C + 1)
    full_part = jax.random.randint(jax.random.fold_in(key, 7), (GRIDS,), 0, PARTS_SIZE)
    part_ids = jnp.arange(PARTS_SIZE, dtype=jnp.int32)[None, :, None]
    counts = jnp.where(part_ids == full_part[:, None, None], C, counts)
    same_grid = jnp.arange(GRIDS, dtype=jnp.int32)[:, None, None] == jnp.arange(GRIDS, dtype=jnp.int32)[None, None, :]
    return jnp.where(same_grid, 0, counts).astype(jnp.int32)


def with_ends(result, rng, least, top_value):
    spot = [jax.random.randint(jax.random.fold_in(rng, axis), (), 0, length) for axis, length in enumerate(result.shape)]
    widest = result.shape.index(max(result.shape))
    neighbour = spot[:widest] + [(spot[widest] + 1) % result.shape[widest]] + spot[widest + 1:]
    return result.at[tuple(spot)].set(least).at[tuple(neighbour)].set(top_value)


def levels(rng, extent, split, low, top_value):
    gain = 1.0
    for dim, shards_of in split:
        draws = jax.random.uniform(jax.random.fold_in(jax.random.fold_in(rng, 6), dim), (shards_of,), jnp.float32, low / len(split), top_value / len(split))
        gain = gain * jnp.repeat(jnp.exp(draws), extent[dim] // shards_of).reshape((-1,) + (1,) * (len(extent) - 1 - dim))
    return gain


def normal_values(own_key, dims, width, most, split=(), held_as=jnp.bfloat16):
    level = levels(own_key, dims, split, -0.22, 0.18) if split else 1.0
    entries = jax.random.normal(own_key, dims, jnp.float32) * width * level
    return jnp.minimum(jnp.maximum(entries, -most), most).astype(held_as)


def setup_inputs(seed: int = 0) -> dict:
    arg_keys = jax.random.split(jax.random.key(seed), 8)
    return {
        "rhs": draw_rhs(jax.random.fold_in(arg_keys[7], 71), 0),
        "blocks": normal_values(arg_keys[1], (GRIDS, ELEMS, NB, W, W), (NB * W) ** -0.5, 0.1875, ((0, 4), (1, 192))),
        "offsets": with_ends(jax.random.randint(arg_keys[2], (GRIDS, ELEMS, NB), 0 - H, H + 1), jax.random.fold_in(arg_keys[2], 1), 0 - H, H).astype(jnp.int32),
        "donor_elem": with_ends(jax.random.randint(arg_keys[3], (GRIDS, PARTS_SIZE, GRIDS, C), 0, E), jax.random.fold_in(arg_keys[3], 1), 0, E - 1).astype(jnp.int32),
        "fringe_elem": with_ends(jax.random.randint(arg_keys[4], (GRIDS, PARTS_SIZE, GRIDS, C), 0, E), jax.random.fold_in(arg_keys[4], 1), 0, E - 1).astype(jnp.int32),
        "donor_weight": jnp.clip(0.25 + 0.75 * jax.random.uniform(arg_keys[5], (GRIDS, PARTS_SIZE, GRIDS, C), jnp.float32) ** levels(arg_keys[5], (GRIDS, PARTS_SIZE, GRIDS, C), ((0, 4), (1, 192)), -0.2, 0.2), 0.25, 1.0),
        "fringe_count": draw_fringe_count(jax.random.fold_in(arg_keys[7], 71), 0),
    }


def one_part(pair):
    return jnp.einsum('ekra,ekab->erb', pair[0].astype(jnp.float32), pair[1].astype(jnp.float32))

def apply_operator(field, blocks, offsets, donor_elem, fringe_elem, donor_weight, fringe_count):
    padded = jnp.pad(field, ((0, 0), (H, H), (0, 0), (0, 0)))
    col_index = jnp.arange(ELEMS, dtype=jnp.int32)[None, :, None] + offsets + H
    taken_cols = jax.vmap(lambda plane, where_from: plane[where_from])(padded, col_index)
    pieces = taken_cols.reshape(GRIDS * PARTS_SIZE, E, NB, R, W)
    block_rows = blocks.reshape(GRIDS * PARTS_SIZE, E, NB, W, W)
    blockpart = lax.map(one_part, (pieces, block_rows)).reshape(GRIDS, ELEMS, R, W)
    flat_field = field.reshape(GRIDS * ELEMS, R, W)
    source_index = jnp.arange(GRIDS, dtype=jnp.int32)[None, None, :, None] * ELEMS + jnp.arange(PARTS_SIZE, dtype=jnp.int32)[None, :, None, None] * E + donor_elem
    picked = flat_field[source_index]
    live_slot = jnp.arange(C, dtype=jnp.int32)[None, None, None, :] < fringe_count[..., None]
    weights = jnp.where(live_slot, donor_weight, jnp.zeros_like(donor_weight))
    hit_target = fringe_elem[..., None] == jnp.arange(E, dtype=jnp.int32)
    spread = jnp.where(hit_target, weights[..., None], jnp.zeros_like(weights[..., None]))
    donorpart = jnp.einsum('hpgce,hpgcrw->hperw', spread, picked.astype(jnp.float32), precision=lax.Precision.HIGHEST).reshape(GRIDS, ELEMS, R, W)
    return (blockpart + donorpart).astype(jnp.bfloat16)

def reference(rhs, blocks, offsets, donor_elem, fringe_elem, donor_weight, fringe_count):
    basis = [rhs]
    field = rhs
    for level in range(S):
        field = apply_operator(field, blocks, offsets, donor_elem, fringe_elem, donor_weight, fringe_count)
        basis.append(field)
    stacked = jnp.stack(basis, axis=2).astype(jnp.float32)
    gram = jnp.einsum('gnkrw,gnlqw->krlq', stacked, stacked, precision=lax.Precision.HIGHEST)
    gram = gram.reshape(COLS, COLS) / (GRIDS * ELEMS * W)
    r_factor = jnp.linalg.cholesky(gram).T
    powers = jnp.stack(basis[1:], axis=2)
    return (powers, r_factor)
```

```python
import functools

import jax
import jax.numpy as jnp
from jax import lax
from jax.experimental import pallas as pl
from jax.experimental.pallas import tpu as pltpu
from jax.sharding import PartitionSpec as P

MESH = pl.DeviceIdType.MESH
HIGH = lax.Precision.HIGHEST
S = 4
Y = 8
SQ = 96


def nt(a, b, precision=None):
    return lax.dot_general(
        a, b, (((1,), (1,)), ((), ())), precision=precision, preferred_element_type=jnp.float32
    )


def nn(a, b, precision=None):
    return lax.dot_general(
        a, b, (((1,), (0,)), ((), ())), precision=precision, preferred_element_type=jnp.float32
    )


def kernel(
    dims,
    offs, delem, felem, dweight, count, rhs_hbm, blk_hbm,
    pow_hbm, r_out,
    V, B, halo, dsend, drecv, idx, coef, pbuf, s1, sy, sz, fin, linv,
    blk_sem, rhs_sem, out_sem, idx_ss, idx_rs, halo_ss, halo_rs, don_ss, don_rs, ar_ss, ar_rs,
):
    G, D, NY, NZ, E, R, W, C, total = dims
    dom, me = lax.axis_index("dom"), lax.axis_index("grid")
    core = dom % 2
    y = (dom // 2) % NY
    z = dom // (2 * NY)
    left, right = (dom + D - 1) % D, (dom + 1) % D
    grids = [(me + j) % G for j in range(G)]
    group = [
        (dom + dc * (1 - 2 * core), grids[j], (core + dc) % 2)
        for j in range(G) for dc in range(2) if (j, dc) != (0, 0)
    ]
    y_order = sorted(range(1, NY), key=lambda d: -min(d, NY - d))
    z_order = sorted(range(1, NZ), key=lambda d: -min(d, NZ - d))
    y_peers = [(z * NY + (y + d) % NY) * 2 + core for d in y_order]
    z_peers = [(((z + d) % NZ) * NY + y) * 2 + core for d in z_order]

    rhs_copy = pltpu.make_async_copy(rhs_hbm, V.at[:, pl.ds(0, R), :], rhs_sem)
    rhs_copy.start()
    blk_copies = [pltpu.make_async_copy(blk_hbm.at[e], B.at[e], blk_sem.at[e]) for e in range(E)]
    for e in [1, 2, 3, 4, 0, 5]:
        blk_copies[e].start()

    barrier = pltpu.get_barrier_semaphore()
    greeted = [(left, me), (right, me)] + [(d, g) for d, g, _ in group]
    greeted += [(d, me) for d in y_peers] + [(d, me) for d in z_peers]
    for d, g in greeted:
        pl.semaphore_signal(barrier, inc=1, device_id=(d, g), device_id_type=MESH)
    pl.semaphore_wait(barrier, len(greeted))

    pending = []

    def send(src, dst, ss, rs, dev, track=True):
        copy = pltpu.make_async_remote_copy(
            src_ref=src, dst_ref=dst, send_sem=ss, recv_sem=rs, device_id=dev, device_id_type=MESH
        )
        copy.start()
        if track:
            pending.append(copy)

    def wait_bytes(ref, sem):
        pltpu.make_async_copy(ref, ref, sem).wait()

    for j in range(1, G):
        send(delem, idx.at[G - 1 - j], idx_ss.at[j - 1], idx_rs.at[G - 1 - j], (dom, grids[j]))

    def rows(k):
        return pl.ds(k * R, R)

    def send_halo(k):
        send(V.at[0, rows(k), :], halo.at[k, 1], halo_ss.at[k, 0], halo_rs.at[k, 1], (left, me))
        send(V.at[E - 1, rows(k), :], halo.at[k, 0], halo_ss.at[k, 1], halo_rs.at[k, 0], (right, me))

    def send_donors(k):
        for j in range(1, G):
            for c in range(C):
                dsend[k, j - 1, c] = V[idx[j - 1, c, me], rows(k), :]
            send(
                dsend.at[k, j - 1], drecv.at[k, G - 1 - j],
                don_ss.at[k, j - 1], don_rs.at[k, G - 1 - j], (dom, grids[j]),
            )

    rhs_copy.wait()
    send_halo(0)

    for j in range(1, G):
        for c in range(C):
            w = jnp.where(c < count[0, grids[j]], dweight[c, grids[j]], 0.0)
            for e in range(E):
                coef[e, (j - 1) * C + c] = jnp.where(felem[c, grids[j]] == e, w, 0.0)

    linv[...] = jnp.zeros_like(linv)
    r_out[...] = jnp.zeros_like(r_out)
    pbuf[...] = jnp.zeros_like(pbuf)

    def taken(e, b, k):
        off = offs[b, e]
        if e == 0:
            own = V[jnp.maximum(off, 0), rows(k), :]
            edge = halo[k, 0]
            edge = jnp.where(dom == 0, jnp.zeros_like(edge), edge)
            return jnp.where(off < 0, edge, own)
        if e == E - 1:
            own = V[e + jnp.minimum(off, 0), rows(k), :]
            edge = halo[k, 1]
            edge = jnp.where(dom == D - 1, jnp.zeros_like(edge), edge)
            return jnp.where(off > 0, edge, own)
        return V[e + off, rows(k), :]

    NBLK = offs.shape[0]

    def product(e, k):
        lhs = jnp.concatenate([taken(e, b, k) for b in range(NBLK)], axis=-1)
        return nn(lhs, B[e])

    def panel(k):
        cols = (k + 1) * R
        acc = sum(nt(V[e, rows(k), :], V[e, pl.ds(0, cols), :]) for e in range(E))
        for h in range(2):
            pbuf[k - 1, h, :, pl.ds(0, cols)] = acc[h * 8:h * 8 + 8, :]
        if k == 1:
            acc = sum(nt(V[e, rows(0), :], V[e, rows(0), :]) for e in range(E))
            for h in range(2):
                pbuf[0, h, :, pl.ds(SQ, R)] = acc[h * 8:h * 8 + 8, :]

    def stage_1(p):
        s1[p, me * 2 + core] = pbuf[p, core]
        for d, g, c in group:
            send(
                pbuf.at[p, c], s1.at[p, me * 2 + core], ar_ss.at[p, 0], ar_rs.at[p, 0], (d, g), False
            )

    def total_of(ref, n):
        parts = [ref[i] for i in range(n)]
        while len(parts) > 1:
            parts = [a + b for a, b in zip(parts[::2], parts[1::2])] + parts[len(parts) & ~1:]
        return parts[0]

    def stage_y(p):
        wait_bytes(s1.at[p, pl.ds(0, 2 * G - 1)], ar_rs.at[p, 0])
        sy[p, y] = total_of(s1.at[p], 2 * G)
        for d in y_peers:
            send(sy.at[p, y], sy.at[p, y], ar_ss.at[p, 1], ar_rs.at[p, 1], (d, me), False)

    def stage_z(p):
        if NY > 1:
            wait_bytes(sy.at[p, pl.ds(0, NY - 1)], ar_rs.at[p, 1])
        sz[p, z] = total_of(sy.at[p], NY)
        for d in z_peers:
            send(sz.at[p, z], sz.at[p, z], ar_ss.at[p, 2], ar_rs.at[p, 2], (d, me), False)

    def stage_core(p):
        if NZ > 1:
            wait_bytes(sz.at[p, pl.ds(0, NZ - 1)], ar_rs.at[p, 2])
        fin[p, core] = total_of(sz.at[p], NZ)
        send(
            fin.at[p, core], fin.at[p, core], ar_ss.at[p, 3], ar_rs.at[p, 3],
            (dom + 1 - 2 * core, me), False,
        )

    def whole(p):
        wait_bytes(fin.at[p, 0], ar_rs.at[p, 3])
        return fin[p].reshape(R, 128) * (1.0 / total)

    lane = lax.broadcasted_iota(jnp.int32, (R, 128), 1)
    sub = lax.broadcasted_iota(jnp.int32, (R, 128), 0)

    def factor(k, pan):
        n = k * R
        rest = 128 - SQ - R
        if k == 0:
            square = jnp.where((lane >= SQ) & (lane < SQ + R), pan, 0.0)
            tab = square + jnp.where(lane == sub, 1.0, 0.0)
        else:
            left_part = jnp.where(lane < n, pan, 0.0)
            low = nt(left_part, linv[...], HIGH)
            placed = jnp.concatenate(
                [jnp.zeros((SQ, 128), jnp.float32), low, jnp.zeros((rest, 128), jnp.float32)], axis=0
            )
            square = pltpu.roll(jnp.where((lane >= n) & (lane < n + R), pan, 0.0), SQ - n, 1)
            tab = square - nt(low, placed, HIGH)
            tab = tab + jnp.where(lane == sub + n, 1.0, 0.0)
            if k < S:
                tab = tab - nn(low, linv[...], HIGH)
            turned = jnp.transpose(low)
            r_out[pl.ds(0, n), pl.ds(n, R)] = turned[:n, :]
        for j in range(R - 1):
            col = jnp.broadcast_to(tab[:, SQ + j:SQ + j + 1], (R, 128))
            mul = jnp.where(sub > j, col / col[j:j + 1, :], 0.0)
            tab = tab - mul * tab[j:j + 1, :]
        diag = jnp.sum(jnp.where(lane == sub + SQ, tab, 0.0), axis=1, keepdims=True)
        tab = tab * (1.0 / jnp.sqrt(diag))
        own = jnp.where((lane >= sub + SQ) & (lane < SQ + R), tab, 0.0)
        r_out[pl.ds(n, R), pl.ds(n, R)] = own[:, SQ:SQ + R]
        if k < S:
            linv[pl.ds(n, R), :] = jnp.where(lane < n + R, tab, 0.0)

    out_copies = []
    advance = {
        1: [],
        2: [(stage_y, 0)],
        3: [(stage_y, 1), (stage_z, 0)],
        4: [(stage_y, 2), (stage_z, 1), (stage_core, 0)],
    }
    for k in range(1, S + 1):
        prev = k - 1
        if k == 1:
            for c in [1, 2, 3, 4]:
                blk_copies[c].wait()
            for j in range(1, G):
                pltpu.make_async_remote_copy(
                    src_ref=delem, dst_ref=idx.at[j - 1], send_sem=idx_ss.at[j - 1],
                    recv_sem=idx_rs.at[j - 1], device_id=(dom, grids[j]), device_id_type=MESH,
                ).wait_recv()
            send_donors(0)
        acc = [None] * E
        for e in range(1, E - 1):
            acc[e] = product(e, prev)
        if k == 1:
            blk_copies[0].wait()
            blk_copies[E - 1].wait()
        for side in range(2):
            wait_bytes(halo.at[prev, side], halo_rs.at[prev, side])
        for e in (0, E - 1):
            acc[e] = product(e, prev)
        for j in range(1, G):
            wait_bytes(drecv.at[prev, j - 1], don_rs.at[prev, j - 1])
        for j in range(1, G):
            for c in range(C):
                donor = drecv[prev, j - 1, c].astype(jnp.float32)
                for e in range(E):
                    acc[e] = acc[e] + coef[e, (j - 1) * C + c] * donor
        for e in range(E):
            V[e, rows(k), :] = acc[e].astype(jnp.bfloat16)
        if k < S:
            send_halo(k)
            send_donors(k)
        copy = pltpu.make_async_copy(
            V.at[:, rows(k), :], pow_hbm.at[:, rows(prev), :], out_sem.at[prev]
        )
        copy.start()
        out_copies.append(copy)
        panel(k)
        stage_1(prev)
        for step, p in advance[k]:
            step(p)

    stage_y(3)
    stage_z(2)
    stage_core(1)
    first = whole(0)
    factor(0, first)
    factor(1, first)
    stage_z(3)
    stage_core(2)
    factor(2, whole(1))
    factor(3, whole(2))
    stage_core(3)
    factor(4, whole(3))

    for copy in out_copies:
        copy.wait()
    for copy in pending:
        copy.wait_send()
    for p in range(S):
        wait_bytes(s1.at[p, pl.ds(0, 2 * G - 1)], ar_ss.at[p, 0])
        if NY > 1:
            wait_bytes(sy.at[p, pl.ds(0, NY - 1)], ar_ss.at[p, 1])
        if NZ > 1:
            wait_bytes(sz.at[p, pl.ds(0, NZ - 1)], ar_ss.at[p, 2])
        wait_bytes(fin.at[p, 0], ar_ss.at[p, 3])


def solution(mesh):
    G, D = mesh.shape["grid"], mesh.shape["dom"]
    NY = Y
    NZ = D // (2 * NY)

    def local(rhs, blocks, offsets, donor_elem, fringe_elem, donor_weight, fringe_count):
        _, E, R, W = rhs.shape
        NB = blocks.shape[2]
        C = donor_elem.shape[3]
        dims = (G, D, NY, NZ, E, R, W, C, G * D * E * W)
        smem = pl.BlockSpec(memory_space=pltpu.SMEM)
        hbm = pl.BlockSpec(memory_space=pl.ANY)
        bf, f32, i32 = jnp.bfloat16, jnp.float32, jnp.int32
        dma = pltpu.SemaphoreType.DMA
        powers, r_factor = pl.pallas_call(
            functools.partial(kernel, dims),
            out_shape=(
                jax.ShapeDtypeStruct((E, S * R, W), bf),
                jax.ShapeDtypeStruct(((S + 1) * R, (S + 1) * R), f32),
            ),
            in_specs=[smem] * 5 + [hbm] * 2,
            out_specs=(hbm, pl.BlockSpec(memory_space=pltpu.VMEM)),
            scratch_shapes=[
                pltpu.VMEM((E, (S + 1) * R, W), bf),
                pltpu.VMEM((E, NB * W, W), bf),
                pltpu.VMEM((S, 2, R, W), bf),
                pltpu.VMEM((S, G - 1, C, R, W), bf),
                pltpu.VMEM((S, G - 1, C, R, W), bf),
                pltpu.SMEM((G - 1, C, G), i32),
                pltpu.SMEM((E, (G - 1) * C), f32),
                pltpu.VMEM((S, 2, 8, 128), f32),
                pltpu.VMEM((S, 2 * G, 8, 128), f32),
                pltpu.VMEM((S, NY, 8, 128), f32),
                pltpu.VMEM((S, NZ, 8, 128), f32),
                pltpu.VMEM((S, 2, 8, 128), f32),
                pltpu.VMEM((128, 128), f32),
                dma((E,)), dma(()), dma((S,)),
                dma((G - 1,)), dma((G - 1,)),
                dma((S, 2)), dma((S, 2)),
                dma((S, G - 1)), dma((S, G - 1)),
                dma((S, 4)), dma((S, 4)),
            ],
            compiler_params=pltpu.CompilerParams(
                collective_id=0, has_side_effects=True, vmem_limit_bytes=32 << 20
            ),
            name="powers_qr",
        )(
            offsets[0].T,
            donor_elem[0, 0].T,
            fringe_elem[0, 0].T,
            donor_weight[0, 0].T,
            fringe_count[0],
            rhs[0],
            blocks.reshape(E, NB * W, W),
        )
        return powers.reshape(1, E, S, R, W), r_factor

    in_specs = (
        P("grid", "dom", None, None),
        P("grid", "dom", None, None, None),
        P("grid", "dom", None),
        P("grid", "dom", None, None),
        P("grid", "dom", None, None),
        P("grid", "dom", None, None),
        P("grid", "dom", None),
    )
    out_specs = (P("grid", "dom", None, None, None), P())
    return jax.shard_map(local, mesh=mesh, in_specs=in_specs, out_specs=out_specs, check_vma=False)
```

```python
import functools

import jax
import jax.numpy as jnp
from jax import lax
from jax.experimental import pallas as pl
from jax.experimental.pallas import tpu as pltpu
from jax.sharding import PartitionSpec as P

MESH = pl.DeviceIdType.MESH
HIGH = lax.Precision.HIGHEST
S = 4
Y = 8
SQ = 96


def nt(a, b, precision=None):
    return lax.dot_general(
        a, b, (((1,), (1,)), ((), ())), precision=precision, preferred_element_type=jnp.float32
    )


def nn(a, b, precision=None):
    return lax.dot_general(
        a, b, (((1,), (0,)), ((), ())), precision=precision, preferred_element_type=jnp.float32
    )


def kernel(
    dims,
    offs_hbm, delem_hbm, felem_hbm, dweight_hbm, count_hbm, rhs_hbm, blk_hbm,
    pow_hbm, r_out,
    offs, delem, felem, dweight, count,
    V, B, halo, dsend, drecv, idx, coef, acc, pbuf, s1, sy, sz, fin, linv,
    tab_sem, blk_sem, rhs_sem, out_sem, idx_ss, idx_rs, halo_ss, halo_rs, don_ss, don_rs, ar_ss, ar_rs,
    far,
):
    G, D, NY, NZ, E, R, W, C, total = dims
    dom, me = lax.axis_index("dom"), lax.axis_index("grid")
    core = dom % 2
    y = (dom // 2) % NY
    z = dom // (2 * NY)
    left, right = (dom + D - 1) % D, (dom + 1) % D
    grids = [(me + j) % G for j in range(G)]
    group = [
        (dom + dc * (1 - 2 * core), grids[j], (core + dc) % 2)
        for j in range(G) for dc in range(2) if (j, dc) != (0, 0)
    ]
    y_order = sorted(range(1, NY), key=lambda d: -min(d, NY - d))
    z_order = sorted(range(1, NZ), key=lambda d: -min(d, NZ - d))
    y_peers = [(z * NY + (y + d) % NY) * 2 + core for d in y_order]
    z_peers = [(((z + d) % NZ) * NY + y) * 2 + core for d in z_order]

    tables = [
        pltpu.make_async_copy(src, dst, tab_sem.at[i])
        for i, (src, dst) in enumerate([
            (delem_hbm, delem), (offs_hbm, offs), (felem_hbm, felem), (dweight_hbm, dweight),
            (count_hbm, count),
        ])
    ]
    for copy in tables:
        copy.start()
    rhs_copy = pltpu.make_async_copy(rhs_hbm, V.at[:, pl.ds(0, R), :], rhs_sem)
    rhs_copy.start()
    blk_copies = [pltpu.make_async_copy(blk_hbm.at[e], B.at[e], blk_sem.at[e]) for e in range(E)]
    for e in [1, 2, 3, 4, 0, 5]:
        blk_copies[e].start()

    barrier = pltpu.get_barrier_semaphore()
    greeted = [(left, me), (right, me)] + [(d, g) for d, g, _ in group]
    rings = [(NY, lambda d: (z * NY + (y + d) % NY) * 2 + core)]
    rings += [(NZ, lambda d: (((z + d) % NZ) * NY + y) * 2 + core)]
    greeted += [(at(d), me) for n, at in rings if n > 1 for d in {1, n - 1}]

    def greet(sem, targets):
        for d, g in targets:
            pl.semaphore_signal(sem, inc=1, device_id=(d, g), device_id_type=MESH)

    greet(barrier, greeted)
    pl.semaphore_wait(barrier, len(greeted))

    words = []
    for i, (n, at) in enumerate(rings):
        steps = [d for d, least in [(1, 3), (2, 5), (2, 9)] if n > least]
        assert n <= 13
        for r, d in enumerate(steps):
            words.append((r, far.at[i, r], [(at(d), me), (at(n - d), me)]))

    def tell(r):
        for when, sem, targets in words:
            if when == r:
                greet(sem, targets)

    def hear(r):
        for when, sem, targets in words:
            if when == r:
                pl.semaphore_wait(sem, len(targets))

    tell(0)

    pending = []

    def send(src, dst, ss, rs, dev, track=True):
        copy = pltpu.make_async_remote_copy(
            src_ref=src, dst_ref=dst, send_sem=ss, recv_sem=rs, device_id=dev, device_id_type=MESH
        )
        copy.start()
        if track:
            pending.append(copy)

    def wait_bytes(ref, sem):
        pltpu.make_async_copy(ref, ref, sem).wait()

    farthest_first = sorted(range(1, G), key=lambda j: -min(j, G - j))
    tables[0].wait()
    for j in farthest_first:
        send(delem, idx.at[G - 1 - j], idx_ss.at[j - 1], idx_rs.at[G - 1 - j], (dom, grids[j]))

    def rows(k):
        return pl.ds(k * R, R)

    def send_halo(k):
        send(V.at[0, rows(k), :], halo.at[k, 1], halo_ss.at[k, 0], halo_rs.at[k, 1], (left, me))
        send(V.at[E - 1, rows(k), :], halo.at[k, 0], halo_ss.at[k, 1], halo_rs.at[k, 0], (right, me))

    def send_donors(k):
        for j in farthest_first:
            for c in range(C):
                dsend[k, j - 1, c] = V[idx[j - 1, c, me], rows(k), :]
            send(
                dsend.at[k, j - 1], drecv.at[k, G - 1 - j],
                don_ss.at[k, j - 1], don_rs.at[k, G - 1 - j], (dom, grids[j]),
            )

    rhs_copy.wait()
    send_halo(0)

    for copy in tables[1:]:
        copy.wait()
    for j in range(1, G):
        for c in range(C):
            w = jnp.where(c < count[0, grids[j]], dweight[c, grids[j]], 0.0)
            for e in range(E):
                coef[e, (j - 1) * C + c] = jnp.where(felem[c, grids[j]] == e, w, 0.0)

    linv[...] = jnp.zeros_like(linv)
    r_out[...] = jnp.zeros_like(r_out)
    pbuf[...] = jnp.zeros_like(pbuf)

    def taken(e, b, k):
        off = offs[b, 0, e]
        if e == 0:
            own = V[jnp.maximum(off, 0), rows(k), :]
            edge = halo[k, 0]
            edge = jnp.where(dom == 0, jnp.zeros_like(edge), edge)
            return jnp.where(off < 0, edge, own)
        if e == E - 1:
            own = V[e + jnp.minimum(off, 0), rows(k), :]
            edge = halo[k, 1]
            edge = jnp.where(dom == D - 1, jnp.zeros_like(edge), edge)
            return jnp.where(off > 0, edge, own)
        return V[e + off, rows(k), :]

    NBLK = offs.shape[0]

    def product(e, k):
        lhs = jnp.concatenate([taken(e, b, k) for b in range(NBLK)], axis=-1)
        return nn(lhs, B[e])

    def panel(k):
        cols = (k + 1) * R
        own = sum(nt(V[e, rows(k), :], V[e, pl.ds(0, cols), :]) for e in range(E))
        for h in range(2):
            pbuf[k - 1, h, :, pl.ds(0, cols)] = own[h * 8:h * 8 + 8, :]
        if k == 1:
            own = sum(nt(V[e, rows(0), :], V[e, rows(0), :]) for e in range(E))
            for h in range(2):
                pbuf[0, h, :, pl.ds(SQ, R)] = own[h * 8:h * 8 + 8, :]

    def stage_1(p):
        s1[p, me * 2 + core] = pbuf[p, core]
        for d, g, c in group:
            send(
                pbuf.at[p, c], s1.at[p, me * 2 + core], ar_ss.at[p, 0], ar_rs.at[p, 0], (d, g), False
            )

    def total_of(ref, n):
        parts = [ref[i] for i in range(n)]
        while len(parts) > 1:
            parts = [a + b for a, b in zip(parts[::2], parts[1::2])] + parts[len(parts) & ~1:]
        return parts[0]

    def stage_y(p):
        wait_bytes(s1.at[p, pl.ds(0, 2 * G - 1)], ar_rs.at[p, 0])
        sy[p, y] = total_of(s1.at[p], 2 * G)
        for d in y_peers:
            send(sy.at[p, y], sy.at[p, y], ar_ss.at[p, 1], ar_rs.at[p, 1], (d, me), False)

    def stage_z(p):
        if NY > 1:
            wait_bytes(sy.at[p, pl.ds(0, NY - 1)], ar_rs.at[p, 1])
        sz[p, z] = total_of(sy.at[p], NY)
        for d in z_peers:
            send(sz.at[p, z], sz.at[p, z], ar_ss.at[p, 2], ar_rs.at[p, 2], (d, me), False)

    def stage_core(p):
        if NZ > 1:
            wait_bytes(sz.at[p, pl.ds(0, NZ - 1)], ar_rs.at[p, 2])
        fin[p, core] = total_of(sz.at[p], NZ)
        send(
            fin.at[p, core], fin.at[p, core], ar_ss.at[p, 3], ar_rs.at[p, 3],
            (dom + 1 - 2 * core, me), False,
        )

    def whole(p):
        wait_bytes(fin.at[p, 0], ar_rs.at[p, 3])
        return fin[p].reshape(R, 128) * (1.0 / total)

    lane = lax.broadcasted_iota(jnp.int32, (R, 128), 1)
    sub = lax.broadcasted_iota(jnp.int32, (R, 128), 0)

    def factor(k, pan):
        n = k * R
        rest = 128 - SQ - R
        if k == 0:
            square = jnp.where((lane >= SQ) & (lane < SQ + R), pan, 0.0)
            tab = square + jnp.where(lane == sub, 1.0, 0.0)
        else:
            left_part = jnp.where(lane < n, pan, 0.0)
            low = nt(left_part, linv[...], HIGH)
            placed = jnp.concatenate(
                [jnp.zeros((SQ, 128), jnp.float32), low, jnp.zeros((rest, 128), jnp.float32)], axis=0
            )
            square = pltpu.roll(jnp.where((lane >= n) & (lane < n + R), pan, 0.0), SQ - n, 1)
            tab = square - nt(low, placed, HIGH)
            tab = tab + jnp.where(lane == sub + n, 1.0, 0.0)
            if k < S:
                tab = tab - nn(low, linv[...], HIGH)
            turned = jnp.transpose(low)
            r_out[pl.ds(0, n), pl.ds(n, R)] = turned[:n, :]
        for j in range(R - 1):
            col = jnp.broadcast_to(tab[:, SQ + j:SQ + j + 1], (R, 128))
            mul = jnp.where(sub > j, col / col[j:j + 1, :], 0.0)
            tab = tab - mul * tab[j:j + 1, :]
        diag = jnp.sum(jnp.where(lane == sub + SQ, tab, 0.0), axis=1, keepdims=True)
        tab = tab * (1.0 / jnp.sqrt(diag))
        own = jnp.where((lane >= sub + SQ) & (lane < SQ + R), tab, 0.0)
        r_out[pl.ds(n, R), pl.ds(n, R)] = own[:, SQ:SQ + R]
        if k < S:
            linv[pl.ds(n, R), :] = jnp.where(lane < n + R, tab, 0.0)

    out_copies = []
    advance = {
        1: [],
        2: [(stage_y, 0)],
        3: [(stage_y, 1), (stage_z, 0)],
        4: [(stage_y, 2), (stage_z, 1), (stage_core, 0)],
    }
    for k in range(1, S + 1):
        prev = k - 1
        if k == 1:
            for c in [1, 2, 3, 4]:
                blk_copies[c].wait()
            for j in range(1, G):
                pltpu.make_async_remote_copy(
                    src_ref=delem, dst_ref=idx.at[j - 1], send_sem=idx_ss.at[j - 1],
                    recv_sem=idx_rs.at[j - 1], device_id=(dom, grids[j]), device_id_type=MESH,
                ).wait_recv()
            send_donors(0)
        for e in range(1, E - 1):
            acc[e] = product(e, prev)
        if k == 1:
            blk_copies[0].wait()
            blk_copies[E - 1].wait()
        for side in range(2):
            wait_bytes(halo.at[prev, side], halo_rs.at[prev, side])
        for e in (0, E - 1):
            acc[e] = product(e, prev)
        for j in range(1, G):
            wait_bytes(drecv.at[prev, j - 1], don_rs.at[prev, j - 1])
        slots = [(j - 1, c) for j in range(1, G) for c in range(C)]
        donor = [drecv[prev, j, c].astype(jnp.float32) for j, c in slots]
        for e in range(E):
            value = acc[e]
            for i in range(len(slots)):
                value = value + coef[e, i] * donor[i]
            V[e, rows(k), :] = value.astype(jnp.bfloat16)
        if k < S:
            send_donors(k)
            send_halo(k)
        copy = pltpu.make_async_copy(
            V.at[:, rows(k), :], pow_hbm.at[:, rows(prev), :], out_sem.at[prev]
        )
        copy.start()
        out_copies.append(copy)
        panel(k)
        stage_1(prev)
        if k < S:
            hear(k - 1)
            tell(k)
        for step, p in advance[k]:
            step(p)

    stage_y(3)
    stage_z(2)
    stage_core(1)
    first = whole(0)
    factor(0, first)
    factor(1, first)
    stage_z(3)
    stage_core(2)
    factor(2, whole(1))
    factor(3, whole(2))
    stage_core(3)
    for copy in out_copies:
        copy.wait()
    for copy in pending:
        copy.wait_send()
    for p in range(S):
        wait_bytes(s1.at[p, pl.ds(0, 2 * G - 1)], ar_ss.at[p, 0])
        if NY > 1:
            wait_bytes(sy.at[p, pl.ds(0, NY - 1)], ar_ss.at[p, 1])
        if NZ > 1:
            wait_bytes(sz.at[p, pl.ds(0, NZ - 1)], ar_ss.at[p, 2])
        wait_bytes(fin.at[p, 0], ar_ss.at[p, 3])
    factor(4, whole(3))


def solution(mesh):
    G, D = mesh.shape["grid"], mesh.shape["dom"]
    NY = Y
    NZ = D // (2 * NY)

    def local(rhs, blocks, offsets, donor_elem, fringe_elem, donor_weight, fringe_count):
        _, E, R, W = rhs.shape
        NB = blocks.shape[2]
        C = donor_elem.shape[3]
        dims = (G, D, NY, NZ, E, R, W, C, G * D * E * W)
        hbm = pl.BlockSpec(memory_space=pltpu.HBM)
        bf, f32, i32 = jnp.bfloat16, jnp.float32, jnp.int32
        dma = pltpu.SemaphoreType.DMA
        powers, r_factor = pl.pallas_call(
            functools.partial(kernel, dims),
            out_shape=(
                jax.ShapeDtypeStruct((E, S * R, W), bf),
                jax.ShapeDtypeStruct(((S + 1) * R, (S + 1) * R), f32),
            ),
            in_specs=[hbm] * 7,
            out_specs=(pl.BlockSpec(memory_space=pl.ANY), pl.BlockSpec(memory_space=pltpu.VMEM)),
            scratch_shapes=[
                pltpu.SMEM((NB, 1, E), i32),
                pltpu.SMEM((C, G), i32),
                pltpu.SMEM((C, G), i32),
                pltpu.SMEM((C, G), f32),
                pltpu.SMEM((1, G), i32),
                pltpu.VMEM((E, (S + 1) * R, W), bf),
                pltpu.VMEM((E, NB * W, W), bf),
                pltpu.VMEM((S, 2, R, W), bf),
                pltpu.VMEM((S, G - 1, C, R, W), bf),
                pltpu.VMEM((S, G - 1, C, R, W), bf),
                pltpu.SMEM((G - 1, C, G), i32),
                pltpu.SMEM((E, (G - 1) * C), f32),
                pltpu.VMEM((E, R, W), f32),
                pltpu.VMEM((S, 2, 8, 128), f32),
                pltpu.VMEM((S, 2 * G, 8, 128), f32),
                pltpu.VMEM((S, NY, 8, 128), f32),
                pltpu.VMEM((S, NZ, 8, 128), f32),
                pltpu.VMEM((S, 2, 8, 128), f32),
                pltpu.VMEM((128, 128), f32),
                dma((5,)), dma((E,)), dma(()), dma((S,)),
                dma((G - 1,)), dma((G - 1,)),
                dma((S, 2)), dma((S, 2)),
                dma((S, G - 1)), dma((S, G - 1)),
                dma((S, 4)), dma((S, 4)),
                pltpu.SemaphoreType.REGULAR((2, 3)),
            ],
            compiler_params=pltpu.CompilerParams(
                collective_id=0, has_side_effects=True, vmem_limit_bytes=67_043_328
            ),
            name="powers_qr",
        )(
            offsets.transpose(2, 0, 1),
            donor_elem[0, 0].T,
            fringe_elem[0, 0].T,
            donor_weight[0, 0].T,
            fringe_count[0],
            rhs[0],
            blocks.reshape(E, NB * W, W),
        )
        return powers.reshape(1, E, S, R, W), r_factor

    in_specs = (
        P("grid", "dom", None, None),
        P("grid", "dom", None, None, None),
        P("grid", "dom", None),
        P("grid", "dom", None, None),
        P("grid", "dom", None, None),
        P("grid", "dom", None, None),
        P("grid", "dom", None),
    )
    out_specs = (P("grid", "dom", None, None, None), P())
    return jax.shard_map(local, mesh=mesh, in_specs=in_specs, out_specs=out_specs, check_vma=False)
```

```python
import functools

import jax
import jax.numpy as jnp
from jax import lax
from jax.experimental import pallas as pl
from jax.experimental.pallas import tpu as pltpu
from jax.sharding import PartitionSpec as P

MESH = pl.DeviceIdType.MESH
HIGH = lax.Precision.HIGHEST
S = 4
Y = 8
SQ = 96


def nt(a, b, precision=None):
    return lax.dot_general(
        a, b, (((1,), (1,)), ((), ())), precision=precision, preferred_element_type=jnp.float32
    )


def nn(a, b, precision=None):
    return lax.dot_general(
        a, b, (((1,), (0,)), ((), ())), precision=precision, preferred_element_type=jnp.float32
    )


def column(table, j):
    return jnp.broadcast_to(table[:, j:j + 1], table.shape)


def eliminate(table, at):
    n = table.shape[0]
    lane = lax.broadcasted_iota(jnp.int32, table.shape, 1)
    sub = lax.broadcasted_iota(jnp.int32, table.shape, 0)
    for j in range(0, n, 2):
        one, two = column(table, at + j), column(table, at + j + 1)
        mul_one = jnp.where(sub > j, one * (1.0 / one[j:j + 1, :]), 0.0)
        table = table - mul_one * table[j:j + 1, :]
        if j + 2 < n:
            two = two - mul_one * one[j + 1:j + 2, :]
            mul_two = jnp.where(sub > j + 1, two * (1.0 / two[j + 1:j + 2, :]), 0.0)
            table = table - mul_two * table[j + 1:j + 2, :]
    pivots = jnp.sum(jnp.where(lane == sub + at, table, 0.0), axis=1, keepdims=True)
    return table * (1.0 / jnp.sqrt(pivots))


def factor(k, pan, linv, r_out):
    R = pan.shape[0]
    n = k * R
    lane = lax.broadcasted_iota(jnp.int32, pan.shape, 1)
    sub = lax.broadcasted_iota(jnp.int32, pan.shape, 0)
    if k:
        left = jnp.where(lane < n, pan, 0.0)
        known = linv[...]
        low = nt(left, known, HIGH)
        r_out[pl.ds(0, n), pl.ds(n, R)] = nt(known, left, HIGH)[:n, :]
    if k == S:
        own = eliminate(pan[:, n:n + R] - nt(low, low, HIGH), 0)
        triangle = lax.broadcasted_iota(jnp.int32, own.shape, 1) >= lax.broadcasted_iota(
            jnp.int32, own.shape, 0
        )
        r_out[pl.ds(n, R), pl.ds(n, R)] = jnp.where(triangle, own, 0.0)
        return
    inside = (lane >= SQ) & (lane < SQ + R)
    table = jnp.where(lane == sub + n, 1.0, 0.0)
    if k == 0:
        table = table + jnp.where(inside, pan, 0.0)
    else:
        placed = jnp.concatenate(
            [jnp.zeros((SQ, S * R), jnp.float32), low, jnp.zeros((128 - SQ - R, S * R), jnp.float32)],
            axis=0,
        )
        square = jnp.where(inside, pltpu.roll(pan, SQ - n, 1), 0.0)
        table = table + square - nt(low, placed, HIGH) - nn(low, known, HIGH)
    table = eliminate(table, SQ)
    own = jnp.where((lane >= sub + SQ) & inside, table, 0.0)
    r_out[pl.ds(n, R), pl.ds(n, R)] = own[:, SQ:SQ + R]
    linv[pl.ds(n, R), :] = jnp.where(lane < n + R, table, 0.0)


def finish(total, pow_vmem, r_part, linv, pan, pow_hbm, r_hbm, r_all, sem):
    powers = pltpu.make_async_copy(pow_vmem, pow_hbm, sem.at[0])
    powers.start()
    r_all[...] = r_part[...]
    factor(S, pan[...].reshape(-1, 128) * (1.0 / total), linv, r_all)
    factors = pltpu.make_async_copy(r_all, r_hbm, sem.at[1])
    factors.start()
    factors.wait()
    powers.wait()


def kernel(
    dims,
    offs_hbm, delem_hbm, felem_hbm, dweight_hbm, count_hbm, rhs_hbm, blk_hbm,
    pow_out, r_out, linv, last,
    offs, delem, felem, dweight, count,
    V, B, halo, dsend, drecv, idx, coef, acc, pbuf, s1, sy, sz, fin,
    tab_sem, blk_sem, rhs_sem, idx_ss, idx_rs, halo_ss, halo_rs, don_ss, don_rs, ar_ss, ar_rs,
    far,
):
    G, D, NY, NZ, E, R, W, C, total = dims
    dom, me = lax.axis_index("dom"), lax.axis_index("grid")
    core = lax.rem(dom, 2)
    y = lax.rem(lax.div(dom, 2), NY)
    z = lax.div(dom, 2 * NY)
    left, right = lax.rem(dom + D - 1, D), lax.rem(dom + 1, D)
    grids = [me] + [lax.rem(me + j, G) for j in range(1, G)]
    group = [
        (dom + dc * (1 - 2 * core), grids[j], core + dc * (1 - 2 * core))
        for j in range(G) for dc in range(2) if (j, dc) != (0, 0)
    ]
    y_order = sorted(range(1, NY), key=lambda d: -min(d, NY - d))
    z_order = sorted(range(1, NZ), key=lambda d: -min(d, NZ - d))
    y_peers = [(z * NY + lax.rem(y + d, NY)) * 2 + core for d in y_order]
    z_peers = [(lax.rem(z + d, NZ) * NY + y) * 2 + core for d in z_order]

    tables = [
        pltpu.make_async_copy(src, dst, tab_sem.at[i])
        for i, (src, dst) in enumerate([
            (delem_hbm, delem), (offs_hbm, offs), (felem_hbm, felem), (dweight_hbm, dweight),
            (count_hbm, count),
        ])
    ]
    for copy in tables:
        copy.start()
    rhs_copy = pltpu.make_async_copy(rhs_hbm, V.at[:, pl.ds(0, R), :], rhs_sem)
    rhs_copy.start()
    blk_copies = [pltpu.make_async_copy(blk_hbm.at[e], B.at[e], blk_sem.at[e]) for e in range(E)]
    for e in [1, 2, 3, 4, 0, 5]:
        blk_copies[e].start()

    barrier = pltpu.get_barrier_semaphore()
    greeted = [(left, me), (right, me)] + [(d, g) for d, g, _ in group]
    rings = [(NY, lambda d: (z * NY + lax.rem(y + d, NY)) * 2 + core)]
    rings += [(NZ, lambda d: (lax.rem(z + d, NZ) * NY + y) * 2 + core)]
    greeted += [(at(d), me) for n, at in rings if n > 1 for d in {1, n - 1}]

    def greet(sem, targets):
        for d, g in targets:
            pl.semaphore_signal(sem, inc=1, device_id=(d, g), device_id_type=MESH)

    greet(barrier, greeted)
    pl.semaphore_wait(barrier, len(greeted))

    words = []
    for i, (n, at) in enumerate(rings):
        steps = [d for d, least in [(1, 3), (2, 5), (2, 9)] if n > least]
        assert n <= 13
        for r, d in enumerate(steps):
            words.append((r, far.at[i, r], [(at(d), me), (at(n - d), me)]))

    def tell(r):
        for when, sem, targets in words:
            if when == r:
                greet(sem, targets)

    def hear(r):
        for when, sem, targets in words:
            if when == r:
                pl.semaphore_wait(sem, len(targets))

    tell(0)

    pending = []

    def send(src, dst, ss, rs, dev, track=True):
        copy = pltpu.make_async_remote_copy(
            src_ref=src, dst_ref=dst, send_sem=ss, recv_sem=rs, device_id=dev, device_id_type=MESH
        )
        copy.start()
        if track:
            pending.append(copy)

    def wait_bytes(ref, sem):
        pltpu.make_async_copy(ref, ref, sem).wait()

    farthest_first = sorted(range(1, G), key=lambda j: -min(j, G - j))
    tables[0].wait()
    for j in farthest_first:
        send(delem, idx.at[G - 1 - j], idx_ss.at[j - 1], idx_rs.at[G - 1 - j], (dom, grids[j]))

    def rows(k):
        return pl.ds(k * R, R)

    def send_halo(k):
        send(V.at[0, rows(k), :], halo.at[k, 1], halo_ss.at[k, 0], halo_rs.at[k, 1], (left, me))
        send(V.at[E - 1, rows(k), :], halo.at[k, 0], halo_ss.at[k, 1], halo_rs.at[k, 0], (right, me))

    def send_donors(k):
        for j in farthest_first:
            for c in range(C):
                dsend[k, j - 1, c] = V[idx[j - 1, c, me], rows(k), :]
            send(
                dsend.at[k, j - 1], drecv.at[k, G - 1 - j],
                don_ss.at[k, j - 1], don_rs.at[k, G - 1 - j], (dom, grids[j]),
            )

    rhs_copy.wait()
    send_halo(0)

    for copy in tables[1:]:
        copy.wait()
    for j in range(1, G):
        for c in range(C):
            w = jnp.where(c < count[0, grids[j]], dweight[c, grids[j]], 0.0)
            for e in range(E):
                coef[e, (j - 1) * C + c] = jnp.where(felem[c, grids[j]] == e, w, 0.0)

    linv[...] = jnp.zeros_like(linv)
    r_out[...] = jnp.zeros_like(r_out)
    pbuf[...] = jnp.zeros_like(pbuf)

    def taken(e, b, k):
        off = offs[b, 0, e]
        if isinstance(e, int) and e == 0:
            own = V[jnp.maximum(off, 0), rows(k), :]
            edge = halo[k, 0]
            edge = jnp.where(dom == 0, jnp.zeros_like(edge), edge)
            return jnp.where(off < 0, edge, own)
        if isinstance(e, int) and e == E - 1:
            own = V[e + jnp.minimum(off, 0), rows(k), :]
            edge = halo[k, 1]
            edge = jnp.where(dom == D - 1, jnp.zeros_like(edge), edge)
            return jnp.where(off > 0, edge, own)
        return V[e + off, rows(k), :]

    NBLK = offs.shape[0]

    def product(e, k):
        lhs = jnp.concatenate([taken(e, b, k) for b in range(NBLK)], axis=-1)
        return nn(lhs, B[e])

    def panel(k):
        cols = (k + 1) * R
        own = sum(nt(V[e, rows(k), :], V[e, pl.ds(0, cols), :]) for e in range(E))
        for h in range(2):
            pbuf[k - 1, h, :, pl.ds(0, cols)] = own[h * 8:h * 8 + 8, :]
        if k == 1:
            own = sum(nt(V[e, rows(0), :], V[e, rows(0), :]) for e in range(E))
            for h in range(2):
                pbuf[0, h, :, pl.ds(SQ, R)] = own[h * 8:h * 8 + 8, :]

    def stage_1(p):
        s1[p, me * 2 + core] = pbuf[p, core]
        for d, g, c in group:
            send(
                pbuf.at[p, c], s1.at[p, me * 2 + core], ar_ss.at[p, 0], ar_rs.at[p, 0], (d, g), False
            )

    def total_of(ref, n):
        parts = [ref[i] for i in range(n)]
        while len(parts) > 1:
            parts = [a + b for a, b in zip(parts[::2], parts[1::2])] + parts[len(parts) & ~1:]
        return parts[0]

    def stage_y(p):
        wait_bytes(s1.at[p, pl.ds(0, 2 * G - 1)], ar_rs.at[p, 0])
        sy[p, y] = total_of(s1.at[p], 2 * G)
        for d in y_peers:
            send(sy.at[p, y], sy.at[p, y], ar_ss.at[p, 1], ar_rs.at[p, 1], (d, me), False)

    def stage_z(p):
        if NY > 1:
            wait_bytes(sy.at[p, pl.ds(0, NY - 1)], ar_rs.at[p, 1])
        sz[p, z] = total_of(sy.at[p], NY)
        for d in z_peers:
            send(sz.at[p, z], sz.at[p, z], ar_ss.at[p, 2], ar_rs.at[p, 2], (d, me), False)

    def stage_core(p):
        if NZ > 1:
            wait_bytes(sz.at[p, pl.ds(0, NZ - 1)], ar_rs.at[p, 2])
        fin[p, core] = total_of(sz.at[p], NZ)
        send(
            fin.at[p, core], fin.at[p, core], ar_ss.at[p, 3], ar_rs.at[p, 3],
            (dom + 1 - 2 * core, me), False,
        )

    def arrived(p):
        wait_bytes(fin.at[p, 0], ar_rs.at[p, 3])

    def whole(p):
        return fin[p].reshape(R, 128) * (1.0 / total)

    advance = {
        1: [],
        2: [(stage_y, 0)],
        3: [(stage_y, 1), (stage_z, 0)],
        4: [(stage_y, 2), (stage_z, 1)],
    }
    for k in range(1, S + 1):
        prev = k - 1
        if k == 1:
            for c in [1, 2, 3, 4]:
                blk_copies[c].wait()
            for j in range(1, G):
                pltpu.make_async_remote_copy(
                    src_ref=delem, dst_ref=idx.at[j - 1], send_sem=idx_ss.at[j - 1],
                    recv_sem=idx_rs.at[j - 1], device_id=(dom, grids[j]), device_id_type=MESH,
                ).wait_recv()
            send_donors(0)
        def inner(i, carry):
            for e in (2 * i + 1, 2 * i + 2):
                acc[e] = product(e, prev)
            return carry

        lax.fori_loop(0, E // 2 - 1, inner, 0)
        if k == 1:
            blk_copies[0].wait()
            blk_copies[E - 1].wait()
        for side, e in ((0, 0), (1, E - 1)):
            wait_bytes(halo.at[prev, side], halo_rs.at[prev, side])
            acc[e] = product(e, prev)
        for j in range(1, G):
            wait_bytes(drecv.at[prev, j - 1], don_rs.at[prev, j - 1])
        slots = [(j - 1, c) for j in range(1, G) for c in range(C)]
        donor = [drecv[prev, j, c].astype(jnp.float32) for j, c in slots]
        for e in (0, E - 1, *range(1, E - 1)):
            value = acc[e]
            for i in range(len(slots)):
                value = value + coef[e, i] * donor[i]
            V[e, rows(k), :] = value.astype(jnp.bfloat16)
            if e == E - 1 and k < S:
                send_halo(k)
        if k < S:
            send_donors(k)
        panel(k)
        stage_1(prev)
        if k < S:
            hear(k - 1)
            tell(k)
        for step, p in advance[k]:
            step(p)
        pow_out[:, rows(prev), :] = V[:, rows(k), :]

    stage_core(0)
    stage_y(3)
    stage_z(2)
    arrived(0)
    factor(0, whole(0), linv, r_out)
    stage_core(1)
    stage_z(3)
    factor(1, whole(0), linv, r_out)
    arrived(1)
    factor(2, whole(1), linv, r_out)
    stage_core(2)
    arrived(2)
    factor(3, whole(2), linv, r_out)
    stage_core(3)
    for copy in pending:
        copy.wait_send()
    for p in range(S):
        wait_bytes(s1.at[p, pl.ds(0, 2 * G - 1)], ar_ss.at[p, 0])
        if NY > 1:
            wait_bytes(sy.at[p, pl.ds(0, NY - 1)], ar_ss.at[p, 1])
        if NZ > 1:
            wait_bytes(sz.at[p, pl.ds(0, NZ - 1)], ar_ss.at[p, 2])
        wait_bytes(fin.at[p, 0], ar_ss.at[p, 3])
    arrived(3)
    last[...] = fin[3]


def solution(mesh):
    G, D = mesh.shape["grid"], mesh.shape["dom"]
    NY = Y
    NZ = D // (2 * NY)

    def local(rhs, blocks, offsets, donor_elem, fringe_elem, donor_weight, fringe_count):
        _, E, R, W = rhs.shape
        NB = blocks.shape[2]
        C = donor_elem.shape[3]
        dims = (G, D, NY, NZ, E, R, W, C, G * D * E * W)
        hbm = pl.BlockSpec(memory_space=pltpu.HBM)
        any_space = pl.BlockSpec(memory_space=pl.ANY)
        vmem = pl.BlockSpec(memory_space=pltpu.VMEM)
        bf, f32, i32 = jnp.bfloat16, jnp.float32, jnp.int32
        dma = pltpu.SemaphoreType.DMA
        state = pl.pallas_call(
            functools.partial(kernel, dims),
            out_shape=(
                pltpu.VMEM((E, S * R, W), bf),
                pltpu.VMEM(((S + 1) * R, (S + 1) * R), f32),
                pltpu.VMEM((S * R, 128), f32),
                pltpu.VMEM((2, 8, 128), f32),
            ),
            in_specs=[hbm] * 7,
            out_specs=(vmem,) * 4,
            scratch_shapes=[
                pltpu.SMEM((NB, 1, E), i32),
                pltpu.SMEM((C, G), i32),
                pltpu.SMEM((C, G), i32),
                pltpu.SMEM((C, G), f32),
                pltpu.SMEM((1, G), i32),
                pltpu.VMEM((E, (S + 1) * R, W), bf),
                pltpu.VMEM((E, NB * W, W), bf),
                pltpu.VMEM((S, 2, R, W), bf),
                pltpu.VMEM((S, G - 1, C, R, W), bf),
                pltpu.VMEM((S, G - 1, C, R, W), bf),
                pltpu.SMEM((G - 1, C, G), i32),
                pltpu.SMEM((E, (G - 1) * C), f32),
                pltpu.VMEM((E, R, W), f32),
                pltpu.VMEM((S, 2, 8, 128), f32),
                pltpu.VMEM((S, 2 * G, 8, 128), f32),
                pltpu.VMEM((S, NY, 8, 128), f32),
                pltpu.VMEM((S, NZ, 8, 128), f32),
                pltpu.VMEM((S, 2, 8, 128), f32),
                dma((5,)), dma((E,)), dma(()),
                dma((G - 1,)), dma((G - 1,)),
                dma((S, 2)), dma((S, 2)),
                dma((S, G - 1)), dma((S, G - 1)),
                dma((S, 4)), dma((S, 4)),
                pltpu.SemaphoreType.REGULAR((2, 3)),
            ],
            compiler_params=pltpu.CompilerParams(
                collective_id=0, has_side_effects=True, vmem_limit_bytes=60 << 20
            ),
            name="powers_qr",
        )(
            offsets.transpose(2, 0, 1),
            donor_elem[0, 0].T,
            fringe_elem[0, 0].T,
            donor_weight[0, 0].T,
            fringe_count[0],
            rhs[0],
            blocks.reshape(E, NB * W, W),
        )
        powers, r_factor = pl.pallas_call(
            functools.partial(finish, G * D * E * W),
            out_shape=(
                jax.ShapeDtypeStruct((E, S * R, W), bf),
                jax.ShapeDtypeStruct(((S + 1) * R, (S + 1) * R), f32),
            ),
            in_specs=[any_space, vmem, vmem, vmem],
            out_specs=(any_space, any_space),
            scratch_shapes=[pltpu.VMEM(((S + 1) * R, (S + 1) * R), f32), dma((2,))],
            compiler_params=pltpu.CompilerParams(vmem_limit_bytes=2 << 20),
            name="finish",
        )(*state)
        return powers.reshape(1, E, S, R, W), r_factor

    in_specs = (
        P("grid", "dom", None, None),
        P("grid", "dom", None, None, None),
        P("grid", "dom", None),
        P("grid", "dom", None, None),
        P("grid", "dom", None, None),
        P("grid", "dom", None, None),
        P("grid", "dom", None),
    )
    out_specs = (P("grid", "dom", None, None, None), P())
    return jax.shard_map(local, mesh=mesh, in_specs=in_specs, out_specs=out_specs, check_vma=False)
```

```python
import functools

import jax
import jax.numpy as jnp
from jax import lax
from jax.experimental import pallas as pl
from jax.experimental.pallas import tpu as pltpu
from jax.sharding import PartitionSpec as P

MESH = pl.DeviceIdType.MESH
HIGH = lax.Precision.HIGHEST
S = 4
Y = 8
SQ = 96


def nt(a, b, precision=None):
    return lax.dot_general(
        a, b, (((1,), (1,)), ((), ())), precision=precision, preferred_element_type=jnp.float32
    )


def nn(a, b, precision=None):
    return lax.dot_general(
        a, b, (((1,), (0,)), ((), ())), precision=precision, preferred_element_type=jnp.float32
    )


def wrap(i, n):
    for shift in range(1, 20):
        power = 1 << shift
        scale = -(-power // n)
        if all(v * scale // power == v // n for v in range(2 * n)):
            return i - n * lax.div(i * scale, power)
    return lax.rem(i, n)


def column(table, j):
    return jnp.broadcast_to(table[:, j:j + 1], table.shape)


def eliminate(table, at):
    n = table.shape[0]
    lane = lax.broadcasted_iota(jnp.int32, table.shape, 1)
    sub = lax.broadcasted_iota(jnp.int32, table.shape, 0)
    for j in range(0, n, 2):
        one, two = column(table, at + j), column(table, at + j + 1)
        mul_one = jnp.where(sub > j, one * (1.0 / one[j:j + 1, :]), 0.0)
        table = table - mul_one * table[j:j + 1, :]
        if j + 2 < n:
            two = two - mul_one * one[j + 1:j + 2, :]
            mul_two = jnp.where(sub > j + 1, two * (1.0 / two[j + 1:j + 2, :]), 0.0)
            table = table - mul_two * table[j + 1:j + 2, :]
    pivots = jnp.sum(jnp.where(lane == sub + at, table, 0.0), axis=1, keepdims=True)
    return table * (1.0 / jnp.sqrt(pivots))


def factor(k, pan, linv, r_out):
    R = pan.shape[0]
    n = k * R
    lane = lax.broadcasted_iota(jnp.int32, pan.shape, 1)
    sub = lax.broadcasted_iota(jnp.int32, pan.shape, 0)
    if k:
        left = jnp.where(lane < n, pan, 0.0)
        known = linv[...]
        low = nt(left, known, HIGH)
        r_out[pl.ds(0, n), pl.ds(n, R)] = nt(known, left, HIGH)[:n, :]
    if k == S:
        own = eliminate(pan[:, n:n + R] - nt(low, low, HIGH), 0)
        triangle = lax.broadcasted_iota(jnp.int32, own.shape, 1) >= lax.broadcasted_iota(
            jnp.int32, own.shape, 0
        )
        r_out[pl.ds(n, R), pl.ds(n, R)] = jnp.where(triangle, own, 0.0)
        return
    inside = (lane >= SQ) & (lane < SQ + R)
    table = jnp.where(lane == sub + n, 1.0, 0.0)
    if k == 0:
        table = table + jnp.where(inside, pan, 0.0)
    else:
        placed = jnp.concatenate(
            [jnp.zeros((SQ, S * R), jnp.float32), low, jnp.zeros((128 - SQ - R, S * R), jnp.float32)],
            axis=0,
        )
        square = jnp.where(inside, pltpu.roll(pan, SQ - n, 1), 0.0)
        table = table + square - nt(low, placed, HIGH) - nn(low, known, HIGH)
    table = eliminate(table, SQ)
    own = jnp.where((lane >= sub + SQ) & inside, table, 0.0)
    r_out[pl.ds(n, R), pl.ds(n, R)] = own[:, SQ:SQ + R]
    linv[pl.ds(n, R), :] = jnp.where(lane < n + R, table, 0.0)


def finish(total, pow_vmem, r_part, linv, pan, pow_hbm, r_hbm, r_all, sem):
    powers = pltpu.make_async_copy(pow_vmem, pow_hbm, sem.at[0])
    powers.start()
    r_all[...] = r_part[...]
    factor(S, pan[...].reshape(-1, 128) * (1.0 / total), linv, r_all)
    factors = pltpu.make_async_copy(r_all, r_hbm, sem.at[1])
    factors.start()
    factors.wait()
    powers.wait()


def kernel(
    dims,
    offs_hbm, delem_hbm, felem_hbm, dweight_hbm, count_hbm, rhs_hbm, blk_hbm,
    pow_out, r_out, linv, last,
    offs, delem, felem, dweight, count,
    V, B, halo, dsend, drecv, idx, coef, acc, pbuf, s1, sy, sz, fin,
    tab_sem, blk_sem, rhs_sem, idx_ss, idx_rs, halo_ss, halo_rs, don_ss, don_rs, ar_ss, ar_rs,
    far,
):
    G, D, NY, NZ, E, R, W, C, total = dims
    dom, me = lax.axis_index("dom"), lax.axis_index("grid")
    core = lax.rem(dom, 2)
    y = lax.rem(lax.div(dom, 2), NY)
    z = lax.div(dom, 2 * NY)
    left, right = wrap(dom + D - 1, D), wrap(dom + 1, D)
    grids = [me] + [wrap(me + j, G) for j in range(1, G)]
    group = [
        (dom + dc * (1 - 2 * core), grids[j])
        for j in range(G) for dc in range(2) if (j, dc) != (0, 0)
    ]
    y_order = sorted(range(1, NY), key=lambda d: -min(d, NY - d))
    z_order = sorted(range(1, NZ), key=lambda d: -min(d, NZ - d))
    y_peers = [(z * NY + wrap(y + d, NY)) * 2 + core for d in y_order]
    z_peers = [(wrap(z + d, NZ) * NY + y) * 2 + core for d in z_order]

    barrier = pltpu.get_barrier_semaphore()
    greeted = [(left, me), (right, me)] + group
    rings = [(NY, lambda d: (z * NY + wrap(y + d, NY)) * 2 + core)]
    rings += [(NZ, lambda d: (wrap(z + d, NZ) * NY + y) * 2 + core)]
    greeted += [(at(d), me) for n, at in rings if n > 1 for d in {1, n - 1}]

    def greet(sem, targets):
        for d, g in targets:
            pl.semaphore_signal(sem, inc=1, device_id=(d, g), device_id_type=MESH)

    greet(barrier, greeted)

    tables = [
        pltpu.make_async_copy(src, dst, tab_sem.at[i])
        for i, (src, dst) in enumerate([
            (delem_hbm, delem), (offs_hbm, offs), (felem_hbm, felem), (dweight_hbm, dweight),
            (count_hbm, count),
        ])
    ]
    for copy in tables:
        copy.start()
    rhs_copy = pltpu.make_async_copy(rhs_hbm, V.at[:, pl.ds(0, R), :], rhs_sem)
    rhs_copy.start()
    blk_copies = [pltpu.make_async_copy(blk_hbm.at[e], B.at[e], blk_sem.at[e]) for e in range(E)]
    for e in [1, 2, 3, 4, 0, 5]:
        blk_copies[e].start()

    pl.semaphore_wait(barrier, len(greeted))

    words = []
    for i, (n, at) in enumerate(rings):
        steps = [d for d, least in [(1, 3), (2, 5), (2, 9)] if n > least]
        assert n <= 13
        for r, d in enumerate(steps):
            words.append((r, far.at[i, r], [(at(d), me), (at(n - d), me)]))

    def tell(r):
        for when, sem, targets in words:
            if when == r:
                greet(sem, targets)

    def hear(r):
        for when, sem, targets in words:
            if when == r:
                pl.semaphore_wait(sem, len(targets))

    tell(0)

    pending = []

    def send(src, dst, ss, rs, dev, track=True):
        copy = pltpu.make_async_remote_copy(
            src_ref=src, dst_ref=dst, send_sem=ss, recv_sem=rs, device_id=dev, device_id_type=MESH
        )
        copy.start()
        if track:
            pending.append(copy)

    def wait_bytes(ref, sem):
        pltpu.make_async_copy(ref, ref, sem).wait()

    farthest_first = sorted(range(1, G), key=lambda j: -min(j, G - j))
    tables[0].wait()
    for j in farthest_first:
        send(delem, idx.at[G - 1 - j], idx_ss.at[j - 1], idx_rs.at[G - 1 - j], (dom, grids[j]))

    def rows(k):
        return pl.ds(k * R, R)

    def send_halo(k):
        send(V.at[0, rows(k), :], halo.at[k, 1], halo_ss.at[k, 0], halo_rs.at[k, 1], (left, me))
        send(V.at[E - 1, rows(k), :], halo.at[k, 0], halo_ss.at[k, 1], halo_rs.at[k, 0], (right, me))

    def send_donors(k):
        for j in farthest_first:
            for c in range(C):
                dsend[k, j - 1, c] = V[idx[j - 1, c, me], rows(k), :]
            send(
                dsend.at[k, j - 1], drecv.at[k, G - 1 - j],
                don_ss.at[k, j - 1], don_rs.at[k, G - 1 - j], (dom, grids[j]),
            )

    rhs_copy.wait()
    send_halo(0)

    for copy in tables[1:]:
        copy.wait()
    for j in range(1, G):
        for c in range(C):
            w = jnp.where(c < count[0, grids[j]], dweight[c, grids[j]], 0.0)
            for e in range(E):
                coef[e, (j - 1) * C + c] = jnp.where(felem[c, grids[j]] == e, w, 0.0)

    linv[...] = jnp.zeros_like(linv)
    r_out[...] = jnp.zeros_like(r_out)
    pbuf[...] = jnp.zeros_like(pbuf)

    def taken(e, b, k):
        off = offs[b, 0, e]
        if isinstance(e, int) and e == 0:
            own = V[jnp.maximum(off, 0), rows(k), :]
            edge = halo[k, 0]
            edge = jnp.where(dom == 0, jnp.zeros_like(edge), edge)
            return jnp.where(off < 0, edge, own)
        if isinstance(e, int) and e == E - 1:
            own = V[e + jnp.minimum(off, 0), rows(k), :]
            edge = halo[k, 1]
            edge = jnp.where(dom == D - 1, jnp.zeros_like(edge), edge)
            return jnp.where(off > 0, edge, own)
        return V[e + off, rows(k), :]

    NBLK = offs.shape[0]

    def product(e, k):
        lhs = jnp.concatenate([taken(e, b, k) for b in range(NBLK)], axis=-1)
        return nn(lhs, B[e])

    def panel(k):
        cols = (k + 1) * R
        own = sum(nt(V[e, rows(k), :], V[e, pl.ds(0, cols), :]) for e in range(E))
        for h in range(2):
            pbuf[k - 1, h, :, pl.ds(0, cols)] = own[h * 8:h * 8 + 8, :]
        if k == 1:
            own = sum(nt(V[e, rows(0), :], V[e, rows(0), :]) for e in range(E))
            for h in range(2):
                pbuf[0, h, :, pl.ds(SQ, R)] = own[h * 8:h * 8 + 8, :]

    def stage_1(p):
        s1[p, me * 2 + core] = pbuf[p]
        for d, g in group:
            send(
                pbuf.at[p], s1.at[p, me * 2 + core], ar_ss.at[p, 0], ar_rs.at[p, 0], (d, g), False
            )

    def total_of(ref, n):
        parts = [ref[i] for i in range(n)]
        while len(parts) > 1:
            parts = [a + b for a, b in zip(parts[::2], parts[1::2])] + parts[len(parts) & ~1:]
        return parts[0]

    def stage_y(p):
        wait_bytes(s1.at[p, pl.ds(0, 2 * G - 1)], ar_rs.at[p, 0])
        sy[p, y] = total_of(s1.at[p], 2 * G)
        for d in y_peers:
            send(sy.at[p, y], sy.at[p, y], ar_ss.at[p, 1], ar_rs.at[p, 1], (d, me), False)

    def stage_z(p):
        if NY > 1:
            wait_bytes(sy.at[p, pl.ds(0, NY - 1)], ar_rs.at[p, 1])
        sz[p, z] = total_of(sy.at[p], NY)
        for d in z_peers:
            send(sz.at[p, z], sz.at[p, z], ar_ss.at[p, 2], ar_rs.at[p, 2], (d, me), False)

    def stage_end(p):
        if NZ > 1:
            wait_bytes(sz.at[p, pl.ds(0, NZ - 1)], ar_rs.at[p, 2])
        fin[p] = total_of(sz.at[p], NZ)

    def whole(p):
        return fin[p].reshape(R, 128) * (1.0 / total)

    advance = {
        1: [],
        2: [(stage_y, 0)],
        3: [(stage_y, 1), (stage_z, 0)],
        4: [(stage_y, 2), (stage_z, 1)],
    }
    for k in range(1, S + 1):
        prev = k - 1
        if k == 1:
            for c in [1, 2, 3, 4]:
                blk_copies[c].wait()
            for j in range(1, G):
                pltpu.make_async_remote_copy(
                    src_ref=delem, dst_ref=idx.at[j - 1], send_sem=idx_ss.at[j - 1],
                    recv_sem=idx_rs.at[j - 1], device_id=(dom, grids[j]), device_id_type=MESH,
                ).wait_recv()
            send_donors(0)
        def inner(i, carry):
            for e in (2 * i + 1, 2 * i + 2):
                acc[e] = product(e, prev)
            return carry

        lax.fori_loop(0, E // 2 - 1, inner, 0)
        if k == 1:
            blk_copies[0].wait()
            blk_copies[E - 1].wait()
        for side, e in ((0, 0), (1, E - 1)):
            wait_bytes(halo.at[prev, side], halo_rs.at[prev, side])
            acc[e] = product(e, prev)
        for j in range(1, G):
            wait_bytes(drecv.at[prev, j - 1], don_rs.at[prev, j - 1])
        slots = [(j - 1, c) for j in range(1, G) for c in range(C)]
        donor = [drecv[prev, j, c].astype(jnp.float32) for j, c in slots]
        for e in (0, E - 1, *range(1, E - 1)):
            value = acc[e]
            for i in range(len(slots)):
                value = value + coef[e, i] * donor[i]
            V[e, rows(k), :] = value.astype(jnp.bfloat16)
            if e == E - 1 and k < S:
                send_halo(k)
        if k < S:
            send_donors(k)
        panel(k)
        stage_1(prev)
        if k < S:
            hear(k - 1)
            tell(k)
        for step, p in advance[k]:
            step(p)
        pow_out[:, rows(prev), :] = V[:, rows(k), :]

    stage_y(3)
    stage_end(0)
    factor(0, whole(0), linv, r_out)
    stage_z(2)
    factor(1, whole(0), linv, r_out)
    stage_z(3)
    stage_end(1)
    factor(2, whole(1), linv, r_out)
    stage_end(2)
    factor(3, whole(2), linv, r_out)
    for copy in pending:
        copy.wait_send()
    for p in range(S):
        wait_bytes(s1.at[p, pl.ds(0, 2 * G - 1)], ar_ss.at[p, 0])
        if NY > 1:
            wait_bytes(sy.at[p, pl.ds(0, NY - 1)], ar_ss.at[p, 1])
        if NZ > 1:
            wait_bytes(sz.at[p, pl.ds(0, NZ - 1)], ar_ss.at[p, 2])
    stage_end(3)
    last[...] = fin[3]


def solution(mesh):
    G, D = mesh.shape["grid"], mesh.shape["dom"]
    NY = Y
    NZ = D // (2 * NY)

    def local(rhs, blocks, offsets, donor_elem, fringe_elem, donor_weight, fringe_count):
        _, E, R, W = rhs.shape
        NB = blocks.shape[2]
        C = donor_elem.shape[3]
        dims = (G, D, NY, NZ, E, R, W, C, G * D * E * W)
        hbm = pl.BlockSpec(memory_space=pltpu.HBM)
        any_space = pl.BlockSpec(memory_space=pl.ANY)
        vmem = pl.BlockSpec(memory_space=pltpu.VMEM)
        bf, f32, i32 = jnp.bfloat16, jnp.float32, jnp.int32
        dma = pltpu.SemaphoreType.DMA
        state = pl.pallas_call(
            functools.partial(kernel, dims),
            out_shape=(
                pltpu.VMEM((E, S * R, W), bf),
                pltpu.VMEM(((S + 1) * R, (S + 1) * R), f32),
                pltpu.VMEM((S * R, 128), f32),
                pltpu.VMEM((2, 8, 128), f32),
            ),
            in_specs=[hbm] * 7,
            out_specs=(vmem,) * 4,
            scratch_shapes=[
                pltpu.SMEM((NB, 1, E), i32),
                pltpu.SMEM((C, G), i32),
                pltpu.SMEM((C, G), i32),
                pltpu.SMEM((C, G), f32),
                pltpu.SMEM((1, G), i32),
                pltpu.VMEM((E, (S + 1) * R, W), bf),
                pltpu.VMEM((E, NB * W, W), bf),
                pltpu.VMEM((S, 2, R, W), bf),
                pltpu.VMEM((S, G - 1, C, R, W), bf),
                pltpu.VMEM((S, G - 1, C, R, W), bf),
                pltpu.SMEM((G - 1, C, G), i32),
                pltpu.SMEM((E, (G - 1) * C), f32),
                pltpu.VMEM((E, R, W), f32),
                pltpu.VMEM((S, 2, 8, 128), f32),
                pltpu.VMEM((S, 2 * G, 2, 8, 128), f32),
                pltpu.VMEM((S, NY, 2, 8, 128), f32),
                pltpu.VMEM((S, NZ, 2, 8, 128), f32),
                pltpu.VMEM((S, 2, 8, 128), f32),
                dma((5,)), dma((E,)), dma(()),
                dma((G - 1,)), dma((G - 1,)),
                dma((S, 2)), dma((S, 2)),
                dma((S, G - 1)), dma((S, G - 1)),
                dma((S, 3)), dma((S, 3)),
                pltpu.SemaphoreType.REGULAR((2, 3)),
            ],
            compiler_params=pltpu.CompilerParams(
                collective_id=0, has_side_effects=True, vmem_limit_bytes=60 << 20
            ),
            name="powers_qr",
        )(
            offsets.transpose(2, 0, 1),
            donor_elem[0, 0].T,
            fringe_elem[0, 0].T,
            donor_weight[0, 0].T,
            fringe_count[0],
            rhs[0],
            blocks.reshape(E, NB * W, W),
        )
        powers, r_factor = pl.pallas_call(
            functools.partial(finish, G * D * E * W),
            out_shape=(
                jax.ShapeDtypeStruct((E, S * R, W), bf),
                jax.ShapeDtypeStruct(((S + 1) * R, (S + 1) * R), f32),
            ),
            in_specs=[any_space, vmem, vmem, vmem],
            out_specs=(any_space, any_space),
            scratch_shapes=[pltpu.VMEM(((S + 1) * R, (S + 1) * R), f32), dma((2,))],
            compiler_params=pltpu.CompilerParams(vmem_limit_bytes=2 << 20),
            name="finish",
        )(*state)
        return powers.reshape(1, E, S, R, W), r_factor

    in_specs = (
        P("grid", "dom", None, None),
        P("grid", "dom", None, None, None),
        P("grid", "dom", None),
        P("grid", "dom", None, None),
        P("grid", "dom", None, None),
        P("grid", "dom", None, None),
        P("grid", "dom", None),
    )
    out_specs = (P("grid", "dom", None, None, None), P())
    return jax.shard_map(local, mesh=mesh, in_specs=in_specs, out_specs=out_specs, check_vma=False)
```

```python
import functools

import jax
import jax.numpy as jnp
from jax import lax
from jax.experimental import pallas as pl
from jax.experimental.pallas import tpu as pltpu
from jax.sharding import PartitionSpec as P

MESH = pl.DeviceIdType.MESH
HIGH = lax.Precision.HIGHEST
S = 4
Y = 8
SQ = 96


def nt(a, b, precision=None):
    return lax.dot_general(
        a, b, (((1,), (1,)), ((), ())), precision=precision, preferred_element_type=jnp.float32
    )


def nn(a, b, precision=None):
    return lax.dot_general(
        a, b, (((1,), (0,)), ((), ())), precision=precision, preferred_element_type=jnp.float32
    )


def wrap(i, n):
    for shift in range(1, 20):
        power = 1 << shift
        scale = -(-power // n)
        if all(v * scale // power == v // n for v in range(2 * n)):
            return i - n * lax.div(i * scale, power)
    return lax.rem(i, n)


def column(table, j):
    return jnp.broadcast_to(table[:, j:j + 1], table.shape)


def eliminate(table, at):
    n = table.shape[0]
    lane = lax.broadcasted_iota(jnp.int32, table.shape, 1)
    sub = lax.broadcasted_iota(jnp.int32, table.shape, 0)
    for j in range(0, n, 2):
        one, two = column(table, at + j), column(table, at + j + 1)
        mul_one = jnp.where(sub > j, one * (1.0 / one[j:j + 1, :]), 0.0)
        table = table - mul_one * table[j:j + 1, :]
        if j + 2 < n:
            two = two - mul_one * one[j + 1:j + 2, :]
            mul_two = jnp.where(sub > j + 1, two * (1.0 / two[j + 1:j + 2, :]), 0.0)
            table = table - mul_two * table[j + 1:j + 2, :]
    pivots = jnp.sum(jnp.where(lane == sub + at, table, 0.0), axis=1, keepdims=True)
    return table * (1.0 / jnp.sqrt(pivots))


def factor(k, pan, linv, r_out):
    R = pan.shape[0]
    n = k * R
    lane = lax.broadcasted_iota(jnp.int32, pan.shape, 1)
    sub = lax.broadcasted_iota(jnp.int32, pan.shape, 0)
    if k:
        left = jnp.where(lane < n, pan, 0.0)
        known = linv[...]
        low = nt(left, known, HIGH)
        r_out[pl.ds(0, n), pl.ds(n, R)] = nt(known, left, HIGH)[:n, :]
    if k == S:
        own = eliminate(pan[:, n:n + R] - nt(low, low, HIGH), 0)
        triangle = lax.broadcasted_iota(jnp.int32, own.shape, 1) >= lax.broadcasted_iota(
            jnp.int32, own.shape, 0
        )
        r_out[pl.ds(n, R), pl.ds(n, R)] = jnp.where(triangle, own, 0.0)
        return
    inside = (lane >= SQ) & (lane < SQ + R)
    table = jnp.where(lane == sub + n, 1.0, 0.0)
    if k == 0:
        table = table + jnp.where(inside, pan, 0.0)
    else:
        placed = jnp.concatenate(
            [jnp.zeros((SQ, S * R), jnp.float32), low, jnp.zeros((128 - SQ - R, S * R), jnp.float32)],
            axis=0,
        )
        square = jnp.where(inside, pltpu.roll(pan, SQ - n, 1), 0.0)
        table = table + square - nt(low, placed, HIGH) - nn(low, known, HIGH)
    table = eliminate(table, SQ)
    own = jnp.where((lane >= sub + SQ) & inside, table, 0.0)
    r_out[pl.ds(n, R), pl.ds(n, R)] = own[:, SQ:SQ + R]
    linv[pl.ds(n, R), :] = jnp.where(lane < n + R, table, 0.0)


def finish(total, pow_vmem, r_part, linv, pan, pow_hbm, r_hbm, r_all, sem):
    powers = pltpu.make_async_copy(pow_vmem, pow_hbm, sem.at[0])
    powers.start()
    r_all[...] = r_part[...]
    factor(S, pan[...].reshape(-1, 128) * (1.0 / total), linv, r_all)
    factors = pltpu.make_async_copy(r_all, r_hbm, sem.at[1])
    factors.start()
    factors.wait()
    powers.wait()


def kernel(
    dims,
    offs_hbm, delem_hbm, felem_hbm, dweight_hbm, count_hbm, rhs_hbm, blk_hbm,
    pow_out, r_out, linv, last,
    offs, delem, felem, dweight, count,
    V, B, halo, dsend, drecv, idx, coef, acc, pbuf, s1, sy, sz, fin,
    tab_sem, blk_sem, rhs_sem, idx_ss, idx_rs, halo_ss, halo_rs, don_ss, don_rs, ar_ss, ar_rs,
    far,
):
    G, D, NY, NZ, E, R, W, C, total = dims
    dom, me = lax.axis_index("dom"), lax.axis_index("grid")
    core = lax.rem(dom, 2)
    y = lax.rem(lax.div(dom, 2), NY)
    z = lax.div(dom, 2 * NY)
    left, right = wrap(dom + D - 1, D), wrap(dom + 1, D)
    grids = [me] + [wrap(me + j, G) for j in range(1, G)]
    group = [
        (dom + dc * (1 - 2 * core), grids[j])
        for j in range(G) for dc in range(2) if (j, dc) != (0, 0)
    ]
    y_order = sorted(range(1, NY), key=lambda d: -min(d, NY - d))
    z_order = sorted(range(1, NZ), key=lambda d: -min(d, NZ - d))
    y_peers = [(z * NY + wrap(y + d, NY)) * 2 + core for d in y_order]
    z_peers = [(wrap(z + d, NZ) * NY + y) * 2 + core for d in z_order]

    tables = [
        pltpu.make_async_copy(src, dst, tab_sem.at[i])
        for i, (src, dst) in enumerate([
            (delem_hbm, delem), (offs_hbm, offs), (felem_hbm, felem), (dweight_hbm, dweight),
            (count_hbm, count),
        ])
    ]
    tables[0].start()
    rhs_copy = pltpu.make_async_copy(rhs_hbm, V.at[:, pl.ds(0, R), :], rhs_sem)
    rhs_copy.start()

    barrier = pltpu.get_barrier_semaphore()
    greeted = [(left, me), (right, me)] + group
    rings = [(NY, lambda d: (z * NY + wrap(y + d, NY)) * 2 + core)]
    rings += [(NZ, lambda d: (wrap(z + d, NZ) * NY + y) * 2 + core)]
    greeted += [(at(d), me) for n, at in rings if n > 1 for d in {1, n - 1}]

    def greet(sem, targets):
        for d, g in targets:
            pl.semaphore_signal(sem, inc=1, device_id=(d, g), device_id_type=MESH)

    greet(barrier, greeted)

    for copy in tables[1:]:
        copy.start()
    blk_copies = [pltpu.make_async_copy(blk_hbm.at[e], B.at[e], blk_sem.at[e]) for e in range(E)]
    for e in [1, 2, 3, 4, 0, 5]:
        blk_copies[e].start()

    pl.semaphore_wait(barrier, len(greeted))

    words = []
    for i, (n, at) in enumerate(rings):
        steps = [d for d, least in [(1, 3), (2, 5), (2, 9)] if n > least]
        assert n <= 13
        for r, d in enumerate(steps):
            words.append((r, far.at[i, r], [(at(d), me), (at(n - d), me)]))

    def tell(r):
        for when, sem, targets in words:
            if when == r:
                greet(sem, targets)

    def hear(r):
        for when, sem, targets in words:
            if when == r:
                pl.semaphore_wait(sem, len(targets))

    pending = []

    def send(src, dst, ss, rs, dev, track=True):
        copy = pltpu.make_async_remote_copy(
            src_ref=src, dst_ref=dst, send_sem=ss, recv_sem=rs, device_id=dev, device_id_type=MESH
        )
        copy.start()
        if track:
            pending.append(copy)

    def wait_bytes(ref, sem):
        pltpu.make_async_copy(ref, ref, sem).wait()

    farthest_first = sorted(range(1, G), key=lambda j: -min(j, G - j))
    tables[0].wait()
    for j in farthest_first:
        send(delem, idx.at[G - 1 - j], idx_ss.at[j - 1], idx_rs.at[G - 1 - j], (dom, grids[j]))

    def rows(k):
        return pl.ds(k * R, R)

    def send_halo(k):
        send(V.at[0, rows(k), :], halo.at[k, 1], halo_ss.at[k, 0], halo_rs.at[k, 1], (left, me))
        send(V.at[E - 1, rows(k), :], halo.at[k, 0], halo_ss.at[k, 1], halo_rs.at[k, 0], (right, me))

    def send_donors(k):
        for j in farthest_first:
            for c in range(C):
                dsend[k, j - 1, c] = V[idx[j - 1, c, me], rows(k), :]
            send(
                dsend.at[k, j - 1], drecv.at[k, G - 1 - j],
                don_ss.at[k, j - 1], don_rs.at[k, G - 1 - j], (dom, grids[j]),
            )

    rhs_copy.wait()
    send_halo(0)
    tell(0)

    for copy in tables[1:]:
        copy.wait()
    for j in range(1, G):
        for c in range(C):
            w = jnp.where(c < count[0, grids[j]], dweight[c, grids[j]], 0.0)
            for e in range(E):
                coef[e, (j - 1) * C + c] = jnp.where(felem[c, grids[j]] == e, w, 0.0)

    linv[...] = jnp.zeros_like(linv)
    r_out[...] = jnp.zeros_like(r_out)
    pbuf[...] = jnp.zeros_like(pbuf)

    def taken(e, b, k):
        off = offs[b, 0, e]
        if isinstance(e, int) and e == 0:
            own = V[jnp.maximum(off, 0), rows(k), :]
            edge = halo[k, 0]
            edge = jnp.where(dom == 0, jnp.zeros_like(edge), edge)
            return jnp.where(off < 0, edge, own)
        if isinstance(e, int) and e == E - 1:
            own = V[e + jnp.minimum(off, 0), rows(k), :]
            edge = halo[k, 1]
            edge = jnp.where(dom == D - 1, jnp.zeros_like(edge), edge)
            return jnp.where(off > 0, edge, own)
        return V[e + off, rows(k), :]

    NBLK = offs.shape[0]

    def product(e, k):
        lhs = jnp.concatenate([taken(e, b, k) for b in range(NBLK)], axis=-1)
        return nn(lhs, B[e])

    def panel(k):
        cols = (k + 1) * R
        own = sum(nt(V[e, rows(k), :], V[e, pl.ds(0, cols), :]) for e in range(E))
        for h in range(2):
            pbuf[k - 1, h, :, pl.ds(0, cols)] = own[h * 8:h * 8 + 8, :]
        if k == 1:
            own = sum(nt(V[e, rows(0), :], V[e, rows(0), :]) for e in range(E))
            for h in range(2):
                pbuf[0, h, :, pl.ds(SQ, R)] = own[h * 8:h * 8 + 8, :]

    def stage_1(p):
        s1[p, me * 2 + core] = pbuf[p]
        for d, g in group:
            send(
                pbuf.at[p], s1.at[p, me * 2 + core], ar_ss.at[p, 0], ar_rs.at[p, 0], (d, g), False
            )

    def total_of(ref, n):
        parts = [ref[i] for i in range(n)]
        while len(parts) > 1:
            parts = [a + b for a, b in zip(parts[::2], parts[1::2])] + parts[len(parts) & ~1:]
        return parts[0]

    def stage_y(p):
        wait_bytes(s1.at[p, pl.ds(0, 2 * G - 1)], ar_rs.at[p, 0])
        sy[p, y] = total_of(s1.at[p], 2 * G)
        for d in y_peers:
            send(sy.at[p, y], sy.at[p, y], ar_ss.at[p, 1], ar_rs.at[p, 1], (d, me), False)

    def stage_z(p):
        if NY > 1:
            wait_bytes(sy.at[p, pl.ds(0, NY - 1)], ar_rs.at[p, 1])
        sz[p, z] = total_of(sy.at[p], NY)
        for d in z_peers:
            send(sz.at[p, z], sz.at[p, z], ar_ss.at[p, 2], ar_rs.at[p, 2], (d, me), False)

    def stage_end(p):
        if NZ > 1:
            wait_bytes(sz.at[p, pl.ds(0, NZ - 1)], ar_rs.at[p, 2])
        fin[p] = total_of(sz.at[p], NZ)

    def whole(p):
        return fin[p].reshape(R, 128) * (1.0 / total)

    advance = {
        1: [],
        2: [(stage_y, 0)],
        3: [(stage_y, 1), (stage_z, 0)],
        4: [(stage_y, 2), (stage_z, 1)],
    }
    for k in range(1, S + 1):
        prev = k - 1
        if k == 1:
            for c in [1, 2, 3, 4]:
                blk_copies[c].wait()
            for j in range(1, G):
                pltpu.make_async_remote_copy(
                    src_ref=delem, dst_ref=idx.at[j - 1], send_sem=idx_ss.at[j - 1],
                    recv_sem=idx_rs.at[j - 1], device_id=(dom, grids[j]), device_id_type=MESH,
                ).wait_recv()
            send_donors(0)
        def inner(i, carry):
            for e in (2 * i + 1, 2 * i + 2):
                acc[e] = product(e, prev)
            return carry

        lax.fori_loop(0, E // 2 - 1, inner, 0)
        if k == 1:
            blk_copies[0].wait()
            blk_copies[E - 1].wait()
        for side, e in ((0, 0), (1, E - 1)):
            wait_bytes(halo.at[prev, side], halo_rs.at[prev, side])
            acc[e] = product(e, prev)
        for j in range(1, G):
            wait_bytes(drecv.at[prev, j - 1], don_rs.at[prev, j - 1])
        slots = [(j - 1, c) for j in range(1, G) for c in range(C)]
        donor = [drecv[prev, j, c].astype(jnp.float32) for j, c in slots]
        for e in (0, E - 1, *range(1, E - 1)):
            value = acc[e]
            for i in range(len(slots)):
                value = value + coef[e, i] * donor[i]
            V[e, rows(k), :] = value.astype(jnp.bfloat16)
            if e == E - 1 and k < S:
                send_halo(k)
        if k < S:
            send_donors(k)
        panel(k)
        stage_1(prev)
        if k < S:
            hear(k - 1)
            tell(k)
        for step, p in advance[k]:
            step(p)
        pow_out[:, rows(prev), :] = V[:, rows(k), :]

    stage_y(3)
    stage_end(0)
    factor(0, whole(0), linv, r_out)
    stage_z(2)
    factor(1, whole(0), linv, r_out)
    stage_z(3)
    stage_end(1)
    factor(2, whole(1), linv, r_out)
    stage_end(2)
    factor(3, whole(2), linv, r_out)
    for copy in pending:
        copy.wait_send()
    for p in range(S):
        wait_bytes(s1.at[p, pl.ds(0, 2 * G - 1)], ar_ss.at[p, 0])
        if NY > 1:
            wait_bytes(sy.at[p, pl.ds(0, NY - 1)], ar_ss.at[p, 1])
        if NZ > 1:
            wait_bytes(sz.at[p, pl.ds(0, NZ - 1)], ar_ss.at[p, 2])
    stage_end(3)
    last[...] = fin[3]


def solution(mesh):
    G, D = mesh.shape["grid"], mesh.shape["dom"]
    NY = Y
    NZ = D // (2 * NY)

    def local(rhs, blocks, offsets, donor_elem, fringe_elem, donor_weight, fringe_count):
        _, E, R, W = rhs.shape
        NB = blocks.shape[2]
        C = donor_elem.shape[3]
        dims = (G, D, NY, NZ, E, R, W, C, G * D * E * W)
        hbm = pl.BlockSpec(memory_space=pltpu.HBM)
        any_space = pl.BlockSpec(memory_space=pl.ANY)
        vmem = pl.BlockSpec(memory_space=pltpu.VMEM)
        bf, f32, i32 = jnp.bfloat16, jnp.float32, jnp.int32
        dma = pltpu.SemaphoreType.DMA
        state = pl.pallas_call(
            functools.partial(kernel, dims),
            out_shape=(
                pltpu.VMEM((E, S * R, W), bf),
                pltpu.VMEM(((S + 1) * R, (S + 1) * R), f32),
                pltpu.VMEM((S * R, 128), f32),
                pltpu.VMEM((2, 8, 128), f32),
            ),
            in_specs=[hbm] * 7,
            out_specs=(vmem,) * 4,
            scratch_shapes=[
                pltpu.SMEM((NB, 1, E), i32),
                pltpu.SMEM((C, G), i32),
                pltpu.SMEM((C, G), i32),
                pltpu.SMEM((C, G), f32),
                pltpu.SMEM((1, G), i32),
                pltpu.VMEM((E, (S + 1) * R, W), bf),
                pltpu.VMEM((E, NB * W, W), bf),
                pltpu.VMEM((S, 2, R, W), bf),
                pltpu.VMEM((S, G - 1, C, R, W), bf),
                pltpu.VMEM((S, G - 1, C, R, W), bf),
                pltpu.SMEM((G - 1, C, G), i32),
                pltpu.SMEM((E, (G - 1) * C), f32),
                pltpu.VMEM((E, R, W), f32),
                pltpu.VMEM((S, 2, 8, 128), f32),
                pltpu.VMEM((S, 2 * G, 2, 8, 128), f32),
                pltpu.VMEM((S, NY, 2, 8, 128), f32),
                pltpu.VMEM((S, NZ, 2, 8, 128), f32),
                pltpu.VMEM((S, 2, 8, 128), f32),
                dma((5,)), dma((E,)), dma(()),
                dma((G - 1,)), dma((G - 1,)),
                dma((S, 2)), dma((S, 2)),
                dma((S, G - 1)), dma((S, G - 1)),
                dma((S, 3)), dma((S, 3)),
                pltpu.SemaphoreType.REGULAR((2, 3)),
            ],
            compiler_params=pltpu.CompilerParams(
                collective_id=0, has_side_effects=True, vmem_limit_bytes=60 << 20
            ),
            name="powers_qr",
        )(
            offsets.transpose(2, 0, 1),
            donor_elem[0, 0].T,
            fringe_elem[0, 0].T,
            donor_weight[0, 0].T,
            fringe_count[0],
            rhs[0],
            blocks.reshape(E, NB * W, W),
        )
        powers, r_factor = pl.pallas_call(
            functools.partial(finish, G * D * E * W),
            out_shape=(
                jax.ShapeDtypeStruct((E, S * R, W), bf),
                jax.ShapeDtypeStruct(((S + 1) * R, (S + 1) * R), f32),
            ),
            in_specs=[any_space, vmem, vmem, vmem],
            out_specs=(any_space, any_space),
            scratch_shapes=[pltpu.VMEM(((S + 1) * R, (S + 1) * R), f32), dma((2,))],
            compiler_params=pltpu.CompilerParams(vmem_limit_bytes=2 << 20),
            name="finish",
        )(*state)
        return powers.reshape(1, E, S, R, W), r_factor

    in_specs = (
        P("grid", "dom", None, None),
        P("grid", "dom", None, None, None),
        P("grid", "dom", None),
        P("grid", "dom", None, None),
        P("grid", "dom", None, None),
        P("grid", "dom", None, None),
        P("grid", "dom", None),
    )
    out_specs = (P("grid", "dom", None, None, None), P())
    return jax.shard_map(local, mesh=mesh, in_specs=in_specs, out_specs=out_specs, check_vma=False)
```
